32 devices in a mesh: row: 2 (over x), col: 4 (over y, core), rhs: 4 (over z).
Axes of the slice: x: 2, y: 2, z: 4, core: 2. Of those that a mesh axis runs over, the one named last changes fastest.
Arguments:
- right_side: float32 [2, 64, 8192], P('row', 'rhs', 'col'), may hold values from -6 to 6
- guess: float32 [2, 64, 8192], P('row', 'rhs', 'col'), may hold values from -6 to 6
- inverse: bfloat16 [2, 8192, 8192], P('row', 'rhs', 'col'), may hold values from -0.0625 to 0.0625
- left_factor: bfloat16 [2, 2, 64, 8192], P('row', None, None, 'col'), may hold values from -0.5 to 0.5
- right_factor: bfloat16 [2, 2, 64, 8192], P('row', None, None, 'col'), may hold values from -0.0625 to 0.0625
- ranks: int32 [2, 2], replicated, may hold values from 16 to 64
Outputs:
- solution: float32 [2, 64, 8192], P('row', 'rhs', 'col')
The draws below stay inside these ranges and needn't reach their ends.
Inputs may be any that keep to these rules, and one draw needn't show every extreme that they name: ranks[i, j] is the rank of the block in block row i and block column j; diagonal entries are not read.
All inputs are finite; a program needn't handle non-finite values.
Results may differ from the reference program's by a relative error of at most 0.008.
Values may be sent and summed in bfloat16 or wider, within the bound.
A program may use at most 128 MiB of HBM per device.

```python
import jax
import jax.numpy as jnp
from jax import lax

M = 8192
K = 64
R = 64
NB = 2


def place_ends(result, rng, low, high):
    longest = result.shape.index(max(result.shape))
    spots = []
    for shift in (0, 1):
        where = [jax.random.randint(jax.random.fold_in(rng, axis), (), 0, length) for axis, length in enumerate(result.shape)]
        where[longest] = (where[longest] + shift) % result.shape[longest]
        spots.append(tuple(where))
    return result.at[spots[0]].set(low).at[spots[1]].set(high)


def block_levels(key, dims, shards, smallest, top_value):
    level, own = 1.0, jax.random.fold_in(key, 6)
    for dim, blocks in shards:
        steps = jnp.exp(jax.random.uniform(jax.random.fold_in(own, dim), (blocks,), jnp.float32, smallest / len(shards), top_value / len(shards)))
        level = level * jnp.repeat(steps, dims[dim] // blocks).reshape([-1 if axis == dim else 1 for axis in range(len(dims))])
    return level


def noise(own_key, extent, spread, bound, cuts=(), kind=jnp.bfloat16):
    factor_of = block_levels(own_key, extent, cuts, -0.22, 0.18) if cuts else 1.0
    drawn = jax.random.normal(own_key, extent, jnp.float32) * spread * factor_of
    return jnp.minimum(jnp.maximum(drawn, -bound), bound).astype(kind)


def setup_inputs(seed: int = 0) -> dict:
    arg_keys = jax.random.split(jax.random.key(seed), 7)
    return {
        "right_side": noise(arg_keys[0], (NB, R, M), 1.0, 6.0, ((0, 2), (1, 4), (2, 4)), jnp.float32),
        "guess": noise(arg_keys[1], (NB, R, M), 1.0, 6.0, ((0, 2), (1, 4), (2, 4)), jnp.float32),
        "inverse": noise(arg_keys[2], (NB, M, M), M ** -0.5, 0.0625, ((0, 2), (1, 4), (2, 4))),
        "left_factor": noise(arg_keys[3], (NB, NB, K, M), (K * NB) ** -0.5, 0.5, ((0, 2), (3, 4))),
        "right_factor": noise(arg_keys[4], (NB, NB, K, M), M ** -0.5, 0.0625, ((0, 2), (3, 4))),
        "ranks": place_ends(jax.random.randint(arg_keys[5], (NB, NB), K // 4, K + 1), jax.random.fold_in(arg_keys[5], 1), K // 4, K).astype(jnp.int32),
    }


def reference(right_side, guess, inverse, left_factor, right_factor, ranks):
    keep = (jnp.arange(K, dtype=jnp.int32)[None, None, :] < ranks[:, :, None]).astype(jnp.float32)
    keep_swap = jnp.transpose(keep, (1, 0, 2))
    right_wide = right_factor.astype(jnp.float32)
    guess_low = lax.optimization_barrier(guess.astype(jnp.bfloat16)).astype(jnp.float32)
    old_coef = jnp.einsum("jrm,jikm->jirk", guess_low, right_wide, precision=lax.Precision.HIGHEST)
    old_coef = (old_coef * keep_swap[:, :, None, :]).astype(jnp.bfloat16)
    solved = []
    new_coef = []
    for t in range(NB):
        coupled = jnp.zeros((R, M), jnp.float32)
        for j in range(NB):
            if j > t:
                coupled = coupled + jnp.dot(old_coef[j, t], left_factor[t, j], preferred_element_type=jnp.float32)
            elif j < t:
                coupled = coupled + jnp.dot(new_coef[j][t], left_factor[t, j], preferred_element_type=jnp.float32)
        residue = (right_side[t] - coupled).astype(jnp.bfloat16)
        current = jnp.dot(residue, inverse[t], preferred_element_type=jnp.float32)
        solved.append(current)
        current_low = lax.optimization_barrier(current.astype(jnp.bfloat16)).astype(jnp.float32)
        coef = jnp.einsum("rm,ikm->irk", current_low, right_wide[t], precision=lax.Precision.HIGHEST)
        new_coef.append((coef * keep[:, t][:, None, :]).astype(jnp.bfloat16))
    return jnp.stack(solved)
```

```python
import functools

import jax
import jax.numpy as jnp
from jax import lax
from jax.experimental import pallas as pl
from jax.experimental.pallas import tpu as pltpu
from jax.sharding import PartitionSpec as P

F32 = jnp.float32
BF16 = jnp.bfloat16
TILE = 512


def dot(a, b):
    return lax.dot_general(a, b, (((1,), (0,)), ((), ())), preferred_element_type=F32)


def dot_t(a, b):
    return lax.dot_general(a, b, (((1,), (1,)), ((), ())), preferred_element_type=F32)


def kernel(
    nb, nc, nz, width,
    rhs_ref, guess_ref, inv_ref, left_ref, right_ref, ranks_ref, out_ref,
    inv, low, x, p_rhs, p_left, oc_part, oc_sum, oc_in, nc_part, nc_recv, nc_sum, nc_in,
    s_out, s_in,
    inv_sem, rhs_send, rhs_recv, left_send, left_recv, sib_send, sib_recv,
    og_send, og_recv, ob_send, ob_recv, ng_send, ng_recv, nb_send, nb_recv, rs_send, rs_recv,
):
    row, col, z = lax.axis_index("row"), lax.axis_index("col"), lax.axis_index("rhs")
    slots, part = low.shape[1:]
    m = inv.shape[2]
    rows = nz * slots
    half = col % 2
    sibling = col + 1 - 2 * half
    diag = col == z
    sent = []

    def remote(src, dst, send, recv, where):
        return pltpu.make_async_remote_copy(
            src_ref=src, dst_ref=dst, send_sem=send, recv_sem=recv,
            device_id=where, device_id_type=pl.DeviceIdType.MESH,
        )

    def start(pred, copy):
        @pl.when(pred)
        def _():
            copy.start()
        sent.append((pred, copy))

    loads = []
    for order in range(2):
        h = half if order == 0 else 1 - half
        load = pltpu.make_async_copy(
            inv_ref.at[0, pl.ds(pl.multiple_of(h * part, part), part)], inv.at[h], inv_sem.at[order]
        )
        load.start()
        loads.append(load)

    barrier = pltpu.get_barrier_semaphore()
    count = nb * nc * nz
    me = (row * nc + col) * nz + z
    for step in range(1, count):
        other = lax.rem(me + step, count)
        pl.semaphore_signal(
            barrier, inc=1,
            device_id=(other // (nc * nz), (other // nz) % nc, other % nz),
            device_id_type=pl.DeviceIdType.MESH,
        )
    for h in range(2):
        low[h] = rhs_ref[0, :, h * part:(h + 1) * part].astype(BF16)
    coef = dot_t(guess_ref[0].astype(BF16), right_ref[0].reshape(nb * width, m))
    oc_part[col] = coef
    pl.semaphore_wait(barrier, count - 1)

    mine = pl.ds(pl.multiple_of(z * slots, slots), slots)
    for c in range(nc):
        start(
            jnp.logical_not(diag & (col == c)),
            remote(low.at[c % 2], x.at[c % 2, mine], rhs_send.at[c], rhs_recv.at[z], (row, c, col)),
        )
    for q in range(nb - 1):
        block = lax.rem(row + 1 + q, nb)
        spot = pl.ds(rows + q * width, width)
        for c in range(nc):
            start(
                diag & (col != c),
                remote(
                    left_ref.at[0, block, :, pl.ds((c % 2) * part, part)],
                    x.at[c % 2, spot], left_send.at[q, c], left_recv.at[q], (row, c, z),
                ),
            )
    for step in range(1, nc):
        other = lax.rem(col + step, nc)
        start(
            row > 0,
            remote(oc_part.at[col], oc_part.at[col], og_send.at[step - 1], og_recv.at[col], (row, other, z)),
        )

    @pl.when(diag)
    def _():
        x[half, mine] = low[half]
        for q in range(nb - 1):
            block = lax.rem(row + 1 + q, nb)
            x[half, rows + q * width:rows + (q + 1) * width] = left_ref[
                0, block, :, pl.ds(pl.multiple_of(half * part, part), part)
            ]

    @pl.when(row > 0)
    def _():
        total = oc_part[col]
        for step in range(1, nc):
            other = lax.rem(col + step, nc)
            remote(
                oc_part.at[other], oc_part.at[other], og_send.at[step - 1], og_recv.at[other], (row, other, z)
            ).wait_recv()
            total = total + oc_part[other]
        lane = lax.broadcasted_iota(jnp.int32, total.shape, 1)
        kept = jnp.zeros_like(total)
        for i in range(nb):
            inside = (lane >= i * width) & (lane < i * width + ranks_ref[i, row])
            kept = jnp.where(inside, total, kept)
        oc_sum[...] = kept.astype(BF16)
    for i in range(nb - 1):
        for zz in range(nz):
            start(
                row > i,
                remote(oc_sum, oc_in.at[row, z], ob_send.at[i, zz], ob_recv.at[row, z], (i, col, zz)),
            )

    for zz in range(nz):
        @pl.when(jnp.logical_not(diag & (z == zz)))
        def _():
            spot = x.at[half, pl.ds(zz * slots, slots)]
            remote(spot, spot, rhs_send.at[0], rhs_recv.at[zz], (row, sibling, z)).wait_recv()

    @pl.when(jnp.logical_not(diag))
    def _():
        for q in range(nb - 1):
            spot = x.at[half, pl.ds(rows + q * width, width)]
            remote(spot, spot, left_send.at[0, 0], left_recv.at[q], (row, sibling, z)).wait_recv()

    swap = remote(x.at[half], x.at[half], sib_send, sib_recv, (row, sibling, z))
    swap.start()

    loads[0].wait()

    def first(i, _):
        cut = pl.ds(pl.multiple_of(i * TILE, TILE), TILE)
        value = dot(x[half], inv[half, :, cut])
        p_rhs[:, cut] = value[:rows]
        p_left[:, cut] = value[rows:]
        return _

    lax.fori_loop(0, m // TILE, first, 0)
    loads[1].wait()
    far = x.at[1 - half]
    remote(far, far, sib_send, sib_recv, (row, sibling, z)).wait_recv()

    def second(i, _):
        cut = pl.ds(pl.multiple_of(i * TILE, TILE), TILE)
        value = dot(x[1 - half], inv[1 - half, :, cut])
        p_rhs[:, cut] += value[:rows]
        p_left[:, cut] += value[rows:]
        return _

    lax.fori_loop(0, m // TILE, second, 0)
    swap.wait_send()

    fold = rows // 2
    piece = fold // nc
    for t in range(nb):
        later = nb - 1 - t
        wide = 2 * later * width

        @pl.when(row == t)
        def _():
            blocks = []
            for q in range(nb - 1):
                j = (t + 1 + q) % nb
                if j > t:
                    for zz in range(nz):
                        spot = oc_in.at[j, zz]
                        remote(spot, spot, ob_send.at[0, 0], ob_recv.at[j, zz], (j, col, zz)).wait_recv()
                    blocks.append(
                        jnp.concatenate(
                            [oc_in[j, zz][:, t * width:(t + 1) * width] for zz in range(nz)], axis=0
                        )
                    )
                else:
                    span = 2 * (nb - 1 - j) * width
                    sums = []
                    for c in range(nc):
                        total = None
                        for zz in range(nz):
                            spot = nc_in.at[j, c, zz, :, pl.ds(0, span)]
                            remote(
                                spot, spot, nb_send.at[0, 0, 0], nb_recv.at[j, c, zz], (j, c, zz)
                            ).wait_recv()
                            term = nc_in[j, c, zz, :, :span]
                            total = term if total is None else total + term
                        sums.append(total)
                    folded = jnp.concatenate(sums, axis=0)
                    at = (t - 1 - j) * width
                    whole = jnp.concatenate(
                        [folded[:, at:at + width], folded[:, span // 2 + at:span // 2 + at + width]], axis=0
                    )
                    lane = lax.broadcasted_iota(jnp.int32, whole.shape, 1)
                    whole = jnp.where(lane < ranks_ref[t, j], whole, jnp.zeros_like(whole))
                    blocks.append(whole.astype(BF16))
            coefs = blocks[0] if nb == 2 else jnp.concatenate(blocks, axis=1)
            p_rhs[...] = p_rhs[...] - dot(coefs, p_left[...].astype(BF16))
            for zz in range(nz):
                s_out[zz] = p_rhs[zz * slots:(zz + 1) * slots].astype(BF16)
            if later:
                value = dot_t(
                    s_out[...].reshape(rows, m), right_ref[0, t + 1:].reshape(later * width, m)
                )
                folded = jnp.concatenate([value[:fold], value[fold:]], axis=1)
                for c in range(nc):
                    nc_part[c, :, :wide] = folded[c * piece:(c + 1) * piece]

        if later:
            for step in range(1, nc):
                other = lax.rem(col + step, nc)
                start(
                    row == t,
                    remote(
                        nc_part.at[other, :, pl.ds(0, wide)], nc_recv.at[col, :, pl.ds(0, wide)],
                        ng_send.at[step - 1], ng_recv.at[col], (row, other, z),
                    ),
                )
        for step in range(1, nz):
            other = lax.rem(z + step, nz)
            start(
                row == t,
                remote(s_out.at[other], s_in.at[z], rs_send.at[step - 1], rs_recv.at[z], (row, col, other)),
            )
        if later:
            @pl.when(row == t)
            def _():
                total = nc_part[col, :, :wide]
                for step in range(1, nc):
                    other = lax.rem(col + step, nc)
                    spot = nc_recv.at[other, :, pl.ds(0, wide)]
                    remote(spot, spot, ng_send.at[0], ng_recv.at[other], (row, other, z)).wait_recv()
                    total = total + nc_recv[other, :, :wide]
                nc_sum[:, :wide] = total
            for i in range(t + 1, nb):
                for c in range(nc):
                    for zz in range(nz):
                        start(
                            row == t,
                            remote(
                                nc_sum.at[:, pl.ds(0, wide)], nc_in.at[t, col, z, :, pl.ds(0, wide)],
                                nb_send.at[i, c, zz], nb_recv.at[t, col, z], (i, c, zz),
                            ),
                        )

    total = p_rhs[mine]
    for step in range(1, nz):
        other = lax.rem(z + step, nz)
        spot = s_in.at[other]
        remote(spot, spot, rs_send.at[0], rs_recv.at[other], (row, col, other)).wait_recv()
        total = total + s_in[other].astype(F32)
    out_ref[0] = total
    for pred, copy in sent:
        @pl.when(pred)
        def _():
            copy.wait_send()


def solution(mesh):
    nb, nc, nz = mesh.shape["row"], mesh.shape["col"], mesh.shape["rhs"]

    def body(right_side, guess, inverse, left_factor, right_factor, ranks):
        slots, m = right_side.shape[1:]
        width = left_factor.shape[2]
        rows = nz * slots
        part = inverse.shape[1] // 2
        deep = rows + (nb - 1) * width
        piece = rows // 2 // nc
        wide = 2 * (nb - 1) * width
        dma = pltpu.SemaphoreType.DMA
        vmem = pl.BlockSpec(memory_space=pltpu.VMEM)
        return pl.pallas_call(
            functools.partial(kernel, nb, nc, nz, width),
            out_shape=jax.ShapeDtypeStruct(right_side.shape, F32),
            in_specs=[
                vmem, vmem, pl.BlockSpec(memory_space=pltpu.HBM), vmem, vmem,
                pl.BlockSpec(memory_space=pltpu.SMEM),
            ],
            out_specs=vmem,
            scratch_shapes=[
                pltpu.VMEM((2, part, m), BF16),
                pltpu.VMEM((2, slots, part), BF16),
                pltpu.VMEM((2, deep, part), BF16),
                pltpu.VMEM((rows, m), F32),
                pltpu.VMEM((deep - rows, m), F32),
                pltpu.VMEM((nc, slots, nb * width), F32),
                pltpu.VMEM((slots, nb * width), BF16),
                pltpu.VMEM((nb, nz, slots, nb * width), BF16),
                pltpu.VMEM((nc, piece, wide), F32),
                pltpu.VMEM((nc, piece, wide), F32),
                pltpu.VMEM((piece, wide), F32),
                pltpu.VMEM((nb, nc, nz, piece, wide), F32),
                pltpu.VMEM((nz, slots, m), BF16),
                pltpu.VMEM((nz, slots, m), BF16),
                dma((2,)),
                dma((nc,)), dma((nz,)),
                dma((nb - 1, nc)), dma((nb - 1,)),
                dma, dma,
                dma((nc - 1,)), dma((nc,)),
                dma((nb - 1, nz)), dma((nb, nz)),
                dma((nc - 1,)), dma((nc,)),
                dma((nb, nc, nz)), dma((nb, nc, nz)),
                dma((nz - 1,)), dma((nz,)),
            ],
            compiler_params=pltpu.CompilerParams(
                collective_id=0, has_side_effects=True, vmem_limit_bytes=60 * 1024 * 1024
            ),
        )(right_side, guess, inverse, left_factor, right_factor, ranks)

    in_specs = (
        P("row", "rhs", "col"),
        P("row", "rhs", "col"),
        P("row", "rhs", "col"),
        P("row", None, None, "col"),
        P("row", None, None, "col"),
        P(),
    )
    out_specs = P("row", "rhs", "col")
    return jax.shard_map(body, mesh=mesh, in_specs=in_specs, out_specs=out_specs, check_vma=False)
```

```python
import functools

import jax
import jax.numpy as jnp
from jax import lax
from jax.experimental import pallas as pl
from jax.experimental.pallas import tpu as pltpu
from jax.sharding import PartitionSpec as P

F32 = jnp.float32
BF16 = jnp.bfloat16
TILE = 512
CHUNKS = 4


def dot(a, b):
    return lax.dot_general(a, b, (((1,), (0,)), ((), ())), preferred_element_type=F32)


def dot_t(a, b):
    return lax.dot_general(a, b, (((1,), (1,)), ((), ())), preferred_element_type=F32)


def kernel(
    nb, nc, nz, width,
    rhs_ref, guess_ref, inv_ref, left_ref, right_ref, ranks_ref, out_ref,
    inv, rhs_v, guess_v, right_v, low, x, p_rhs, p_left, p_low, oc_part, oc_sum, oc_in, nc_part, nc_recv, nc_sum, nc_in,
    s_out, s_in,
    inv_sem, in_sem, own_sem, rhs_send, rhs_recv, left_send, left_recv, sib_send, sib_recv,
    og_send, og_recv, ob_send, ob_recv, ng_send, ng_recv, nb_send, nb_recv, rs_send, rs_recv,
):
    row, col, z = lax.axis_index("row"), lax.axis_index("col"), lax.axis_index("rhs")
    slots, part = low.shape[1:]
    m = inv.shape[2]
    rows = nz * slots
    half = col % 2
    sibling = col + 1 - 2 * half
    diag = col == z
    sent = []

    def remote(src, dst, send, recv, where):
        return pltpu.make_async_remote_copy(
            src_ref=src, dst_ref=dst, send_sem=send, recv_sem=recv,
            device_id=where, device_id_type=pl.DeviceIdType.MESH,
        )

    def start(pred, copy):
        @pl.when(pred)
        def _():
            copy.start()
        sent.append((pred, copy))

    barrier = pltpu.get_barrier_semaphore()
    count = nb * nc * nz
    me = (row * nc + col) * nz + z
    for step in range(1, count):
        other = lax.rem(me + step, count)
        pl.semaphore_signal(
            barrier, inc=1,
            device_id=(other // (nc * nz), (other // nz) % nc, other % nz),
            device_id_type=pl.DeviceIdType.MESH,
        )
    early = [
        pltpu.make_async_copy(src, dst, in_sem.at[i])
        for i, (src, dst) in enumerate(
            ((rhs_ref.at[0], rhs_v), (guess_ref.at[0], guess_v), (right_ref.at[0], right_v))
        )
    ]
    for load in early:
        load.start()
    loads = []
    for order in range(2):
        h = half if order == 0 else 1 - half
        load = pltpu.make_async_copy(
            inv_ref.at[0, pl.ds(pl.multiple_of(h * part, part), part)], inv.at[h], inv_sem.at[order]
        )
        load.start()
        loads.append(load)

    early[0].wait()
    for h in range(2):
        low[h] = rhs_v[:, h * part:(h + 1) * part].astype(BF16)
    early[1].wait()
    early[2].wait()
    coef = dot_t(guess_v[...].astype(BF16), right_v[...].reshape(nb * width, m))
    oc_part[col] = coef
    pl.semaphore_wait(barrier, count - 1)

    for step in range(1, nc):
        other = lax.rem(col + step, nc)
        start(
            row > 0,
            remote(oc_part.at[col], oc_part.at[col], og_send.at[step - 1], og_recv.at[col], (row, other, z)),
        )

    mine = pl.ds(pl.multiple_of(z * slots, slots), slots)
    for c in range(nc):
        start(
            jnp.logical_not(diag & (col == c)),
            remote(low.at[c % 2], x.at[c % 2, mine], rhs_send.at[c], rhs_recv.at[z], (row, c, col)),
        )
    for q in range(nb - 1):
        block = lax.rem(row + 1 + q, nb)
        spot = pl.ds(rows + q * width, width)
        for c in range(nc):
            start(
                diag & (col != c),
                remote(
                    left_ref.at[0, block, :, pl.ds((c % 2) * part, part)],
                    x.at[c % 2, spot], left_send.at[q, c], left_recv.at[q], (row, c, z),
                ),
            )
    def own(q):
        return pltpu.make_async_copy(
            left_ref.at[0, lax.rem(row + 1 + q, nb), :, pl.ds(pl.multiple_of(half * part, part), part)],
            x.at[half, pl.ds(rows + q * width, width)], own_sem.at[q],
        )

    @pl.when(diag)
    def _():
        for q in range(nb - 1):
            own(q).start()
        x[half, mine] = low[half]

    @pl.when(row > 0)
    def _():
        total = oc_part[col]
        for step in range(1, nc):
            other = lax.rem(col + step, nc)
            remote(
                oc_part.at[other], oc_part.at[other], og_send.at[step - 1], og_recv.at[other], (row, other, z)
            ).wait_recv()
            total = total + oc_part[other]
        lane = lax.broadcasted_iota(jnp.int32, total.shape, 1)
        kept = jnp.zeros_like(total)
        for i in range(nb):
            inside = (lane >= i * width) & (lane < i * width + ranks_ref[i, row])
            kept = jnp.where(inside, total, kept)
        oc_sum[...] = kept.astype(BF16)
    for i in range(nb - 1):
        for zz in range(nz):
            start(
                row > i,
                remote(oc_sum, oc_in.at[row, z], ob_send.at[i, zz], ob_recv.at[row, z], (i, col, zz)),
            )

    for zz in range(nz):
        @pl.when(jnp.logical_not(diag & (z == zz)))
        def _():
            spot = x.at[half, pl.ds(zz * slots, slots)]
            remote(spot, spot, rhs_send.at[0], rhs_recv.at[zz], (row, sibling, z)).wait_recv()

    @pl.when(diag)
    def _():
        for q in range(nb - 1):
            own(q).wait()

    @pl.when(jnp.logical_not(diag))
    def _():
        for q in range(nb - 1):
            spot = x.at[half, pl.ds(rows + q * width, width)]
            remote(spot, spot, left_send.at[0, 0], left_recv.at[q], (row, sibling, z)).wait_recv()

    swap = remote(x.at[half], x.at[half], sib_send, sib_recv, (row, sibling, z))
    swap.start()

    loads[0].wait()

    def first(i, _):
        cut = pl.ds(pl.multiple_of(i * TILE, TILE), TILE)
        value = dot(x[half], inv[half, :, cut])
        p_rhs[:, cut] = value[:rows]
        p_left[:, cut] = value[rows:]
        return _

    lax.fori_loop(0, m // TILE, first, 0)
    loads[1].wait()
    far = x.at[1 - half]
    remote(far, far, sib_send, sib_recv, (row, sibling, z)).wait_recv()

    def second(i, _):
        cut = pl.ds(pl.multiple_of(i * TILE, TILE), TILE)
        value = dot(x[1 - half], inv[1 - half, :, cut])
        p_rhs[:, cut] += value[:rows]
        p_low[:, cut] = (p_left[:, cut] + value[rows:]).astype(BF16)
        return _

    lax.fori_loop(0, m // TILE, second, 0)
    swap.wait_send()

    fold = rows // 2
    piece = fold // nc
    span_m = m // CHUNKS
    others = [lax.rem(z + step, nz) for step in range(1, nz)]

    def pieces(ch):
        return [
            remote(
                s_out.at[ch, other], s_in.at[ch, z], rs_send.at[ch, i], rs_recv.at[ch, z], (row, col, other)
            )
            for i, other in enumerate(others)
        ]

    def scatter(t, ch):
        for copy in pieces(ch):
            copy.start()

    for t in range(nb):
        later = nb - 1 - t
        wide = 2 * later * width

        @pl.when(row == t)
        def _():
            blocks = []
            for q in range(nb - 1):
                j = (t + 1 + q) % nb
                if j > t:
                    for zz in range(nz):
                        spot = oc_in.at[j, zz]
                        remote(spot, spot, ob_send.at[0, 0], ob_recv.at[j, zz], (j, col, zz)).wait_recv()
                    blocks.append(
                        jnp.concatenate(
                            [oc_in[j, zz][:, t * width:(t + 1) * width] for zz in range(nz)], axis=0
                        )
                    )
                else:
                    span = 2 * (nb - 1 - j) * width
                    sums = []
                    for c in range(nc):
                        total = None
                        for zz in range(nz):
                            spot = nc_in.at[j, c, zz, :, pl.ds(0, span)]
                            remote(
                                spot, spot, nb_send.at[0, 0, 0], nb_recv.at[j, c, zz], (j, c, zz)
                            ).wait_recv()
                            term = nc_in[j, c, zz, :, :span]
                            total = term if total is None else total + term
                        sums.append(total)
                    folded = jnp.concatenate(sums, axis=0)
                    at = (t - 1 - j) * width
                    whole = jnp.concatenate(
                        [folded[:, at:at + width], folded[:, span // 2 + at:span // 2 + at + width]], axis=0
                    )
                    lane = lax.broadcasted_iota(jnp.int32, whole.shape, 1)
                    whole = jnp.where(lane < ranks_ref[t, j], whole, jnp.zeros_like(whole))
                    blocks.append(whole.astype(BF16))
            coefs = blocks[0] if nb == 2 else jnp.concatenate(blocks, axis=1)
            value = None
            for ch in range(CHUNKS):
                cut = slice(ch * span_m, (ch + 1) * span_m)
                now = p_rhs[:, cut] - dot(coefs, p_low[:, cut])
                p_rhs[:, cut] = now
                now = now.astype(BF16)
                for zz in range(nz):
                    s_out[ch, zz] = now[zz * slots:(zz + 1) * slots]
                if later:
                    term = dot_t(now, right_v[t + 1:, :, cut].reshape(later * width, span_m))
                    value = term if value is None else value + term
                else:
                    scatter(t, ch)
            if later:
                folded = jnp.concatenate([value[:fold], value[fold:]], axis=1)
                for c in range(nc):
                    nc_part[c, :, :wide] = folded[c * piece:(c + 1) * piece]

        if later:
            for step in range(1, nc):
                other = lax.rem(col + step, nc)
                start(
                    row == t,
                    remote(
                        nc_part.at[other, :, pl.ds(0, wide)], nc_recv.at[col, :, pl.ds(0, wide)],
                        ng_send.at[step - 1], ng_recv.at[col], (row, other, z),
                    ),
                )
        if later:
            @pl.when(row == t)
            def _():
                total = nc_part[col, :, :wide]
                for step in range(1, nc):
                    other = lax.rem(col + step, nc)
                    spot = nc_recv.at[other, :, pl.ds(0, wide)]
                    remote(spot, spot, ng_send.at[0], ng_recv.at[other], (row, other, z)).wait_recv()
                    total = total + nc_recv[other, :, :wide]
                nc_sum[:, :wide] = total
            for i in range(t + 1, nb):
                for c in range(nc):
                    for zz in range(nz):
                        start(
                            row == t,
                            remote(
                                nc_sum.at[:, pl.ds(0, wide)], nc_in.at[t, col, z, :, pl.ds(0, wide)],
                                nb_send.at[i, c, zz], nb_recv.at[t, col, z], (i, c, zz),
                            ),
                        )

            @pl.when(row == t)
            def _():
                for ch in range(CHUNKS):
                    scatter(t, ch)

    for ch in range(CHUNKS):
        cut = slice(ch * span_m, (ch + 1) * span_m)
        total = p_rhs[mine, cut]
        for other in others:
            spot = s_in.at[ch, other]
            remote(spot, spot, rs_send.at[0, 0], rs_recv.at[ch, other], (row, col, other)).wait_recv()
            total = total + s_in[ch, other].astype(F32)
        out_ref[0, :, cut] = total
    for ch in range(CHUNKS):
        for copy in pieces(ch):
            copy.wait_send()
    for pred, copy in sent:
        @pl.when(pred)
        def _():
            copy.wait_send()


def solution(mesh):
    nb, nc, nz = mesh.shape["row"], mesh.shape["col"], mesh.shape["rhs"]

    def body(right_side, guess, inverse, left_factor, right_factor, ranks):
        slots, m = right_side.shape[1:]
        width = left_factor.shape[2]
        rows = nz * slots
        part = inverse.shape[1] // 2
        deep = rows + (nb - 1) * width
        piece = rows // 2 // nc
        wide = 2 * (nb - 1) * width
        dma = pltpu.SemaphoreType.DMA
        hbm = pl.BlockSpec(memory_space=pltpu.HBM)
        vmem = pl.BlockSpec(memory_space=pltpu.VMEM)
        return pl.pallas_call(
            functools.partial(kernel, nb, nc, nz, width),
            out_shape=jax.ShapeDtypeStruct(right_side.shape, F32),
            in_specs=[
                hbm, hbm, hbm, hbm, hbm,
                pl.BlockSpec(memory_space=pltpu.SMEM),
            ],
            out_specs=vmem,
            scratch_shapes=[
                pltpu.VMEM((2, part, m), BF16),
                pltpu.VMEM((slots, m), F32),
                pltpu.VMEM((slots, m), F32),
                pltpu.VMEM((nb, width, m), BF16),
                pltpu.VMEM((2, slots, part), BF16),
                pltpu.VMEM((2, deep, part), BF16),
                pltpu.VMEM((rows, m), F32),
                pltpu.VMEM((deep - rows, m), F32),
                pltpu.VMEM((deep - rows, m), BF16),
                pltpu.VMEM((nc, slots, nb * width), F32),
                pltpu.VMEM((slots, nb * width), BF16),
                pltpu.VMEM((nb, nz, slots, nb * width), BF16),
                pltpu.VMEM((nc, piece, wide), F32),
                pltpu.VMEM((nc, piece, wide), F32),
                pltpu.VMEM((piece, wide), F32),
                pltpu.VMEM((nb, nc, nz, piece, wide), F32),
                pltpu.VMEM((CHUNKS, nz, slots, m // CHUNKS), BF16),
                pltpu.VMEM((CHUNKS, nz, slots, m // CHUNKS), BF16),
                dma((2,)), dma((3,)), dma((nb - 1,)),
                dma((nc,)), dma((nz,)),
                dma((nb - 1, nc)), dma((nb - 1,)),
                dma, dma,
                dma((nc - 1,)), dma((nc,)),
                dma((nb - 1, nz)), dma((nb, nz)),
                dma((nc - 1,)), dma((nc,)),
                dma((nb, nc, nz)), dma((nb, nc, nz)),
                dma((CHUNKS, nz - 1)), dma((CHUNKS, nz)),
            ],
            compiler_params=pltpu.CompilerParams(
                collective_id=0, has_side_effects=True, vmem_limit_bytes=60 * 1024 * 1024
            ),
        )(right_side, guess, inverse, left_factor, right_factor, ranks)

    in_specs = (
        P("row", "rhs", "col"),
        P("row", "rhs", "col"),
        P("row", "rhs", "col"),
        P("row", None, None, "col"),
        P("row", None, None, "col"),
        P(),
    )
    out_specs = P("row", "rhs", "col")
    return jax.shard_map(body, mesh=mesh, in_specs=in_specs, out_specs=out_specs, check_vma=False)
```

```python
import functools

import jax
import jax.numpy as jnp
from jax import lax
from jax.experimental import pallas as pl
from jax.experimental.pallas import tpu as pltpu
from jax.sharding import PartitionSpec as P

F32 = jnp.float32
BF16 = jnp.bfloat16
TILE = 512
CHUNKS = 4


def dot(a, b):
    return lax.dot_general(a, b, (((1,), (0,)), ((), ())), preferred_element_type=F32)


def dot_t(a, b):
    return lax.dot_general(a, b, (((1,), (1,)), ((), ())), preferred_element_type=F32)


def kernel(
    nb, nc, nz, width,
    rhs_ref, guess_ref, inv_ref, left_ref, right_ref, ranks_ref, out_ref,
    inv, rhs_v, guess_v, right_v, low, x, p_rhs, p_left, p_low, p_sum, w_in,
    coef_v, f_out, f_in, oc_part, oc_sum, oc_in, nc_part, nc_recv, nc_sum, nc_in,
    s_out, s_in,
    inv_sem, in_sem, own_sem, rhs_send, rhs_recv, left_send, left_recv, sib_send, sib_recv,
    og_send, og_recv, ob_send, ob_recv, ng_send, ng_recv, nb_send, nb_recv, rs_send, rs_recv,
    w_send, w_recv, f_send, f_recv,
):
    row, col, z = lax.axis_index("row"), lax.axis_index("col"), lax.axis_index("rhs")
    slots, part = low.shape[1:]
    m = inv.shape[2]
    rows = nz * slots
    half = col % 2
    sibling = col + 1 - 2 * half
    diag = col == z
    sent = []

    def remote(src, dst, send, recv, where):
        return pltpu.make_async_remote_copy(
            src_ref=src, dst_ref=dst, send_sem=send, recv_sem=recv,
            device_id=where, device_id_type=pl.DeviceIdType.MESH,
        )

    def start(pred, copy):
        @pl.when(pred)
        def _():
            copy.start()
        sent.append((pred, copy))

    barrier = pltpu.get_barrier_semaphore()
    count = nb * nc * nz
    me = (row * nc + col) * nz + z
    for step in range(1, count):
        other = lax.rem(me + step, count)
        pl.semaphore_signal(
            barrier, inc=1,
            device_id=(other // (nc * nz), (other // nz) % nc, other % nz),
            device_id_type=pl.DeviceIdType.MESH,
        )
    early = [
        pltpu.make_async_copy(src, dst, in_sem.at[i])
        for i, (src, dst) in enumerate(
            ((rhs_ref.at[0], rhs_v), (guess_ref.at[0], guess_v), (right_ref.at[0], right_v))
        )
    ]
    for load in early:
        load.start()
    loads = []
    for order in range(2):
        h = half if order == 0 else 1 - half
        load = pltpu.make_async_copy(
            inv_ref.at[0, pl.ds(pl.multiple_of(h * part, part), part)], inv.at[h], inv_sem.at[order]
        )
        load.start()
        loads.append(load)

    early[0].wait()
    for h in range(2):
        low[h] = rhs_v[:, h * part:(h + 1) * part].astype(BF16)
    early[1].wait()
    early[2].wait()
    coef = dot_t(guess_v[...].astype(BF16), right_v[...].reshape(nb * width, m))
    oc_part[col] = coef
    pl.semaphore_wait(barrier, count - 1)

    for step in range(1, nc):
        other = lax.rem(col + step, nc)
        start(
            row > 0,
            remote(oc_part.at[col], oc_part.at[col], og_send.at[step - 1], og_recv.at[col], (row, other, z)),
        )

    mine = pl.ds(pl.multiple_of(z * slots, slots), slots)
    for c in range(nc):
        start(
            jnp.logical_not(diag & (col == c)),
            remote(low.at[c % 2], x.at[c % 2, mine], rhs_send.at[c], rhs_recv.at[z], (row, c, col)),
        )
    for q in range(nb - 1):
        block = lax.rem(row + 1 + q, nb)
        spot = pl.ds(rows + q * width, width)
        for c in range(nc):
            start(
                diag & (col != c),
                remote(
                    left_ref.at[0, block, :, pl.ds((c % 2) * part, part)],
                    x.at[c % 2, spot], left_send.at[q, c], left_recv.at[q], (row, c, z),
                ),
            )
    def own(q):
        return pltpu.make_async_copy(
            left_ref.at[0, lax.rem(row + 1 + q, nb), :, pl.ds(pl.multiple_of(half * part, part), part)],
            x.at[half, pl.ds(rows + q * width, width)], own_sem.at[q],
        )

    @pl.when(diag)
    def _():
        for q in range(nb - 1):
            own(q).start()
        x[half, mine] = low[half]

    @pl.when(row > 0)
    def _():
        total = oc_part[col]
        for step in range(1, nc):
            other = lax.rem(col + step, nc)
            remote(
                oc_part.at[other], oc_part.at[other], og_send.at[step - 1], og_recv.at[other], (row, other, z)
            ).wait_recv()
            total = total + oc_part[other]
        lane = lax.broadcasted_iota(jnp.int32, total.shape, 1)
        kept = jnp.zeros_like(total)
        for i in range(nb):
            inside = (lane >= i * width) & (lane < i * width + ranks_ref[i, row])
            kept = jnp.where(inside, total, kept)
        oc_sum[...] = kept.astype(BF16)
    for i in range(nb - 1):
        for zz in range(nz):
            start(
                row > i,
                remote(oc_sum, oc_in.at[row, z], ob_send.at[i, zz], ob_recv.at[row, z], (i, col, zz)),
            )

    for zz in range(nz):
        @pl.when(jnp.logical_not(diag & (z == zz)))
        def _():
            spot = x.at[half, pl.ds(zz * slots, slots)]
            remote(spot, spot, rhs_send.at[0], rhs_recv.at[zz], (row, sibling, z)).wait_recv()

    @pl.when(diag)
    def _():
        for q in range(nb - 1):
            own(q).wait()

    @pl.when(jnp.logical_not(diag))
    def _():
        for q in range(nb - 1):
            spot = x.at[half, pl.ds(rows + q * width, width)]
            remote(spot, spot, left_send.at[0, 0], left_recv.at[q], (row, sibling, z)).wait_recv()

    swap = remote(x.at[half], x.at[half], sib_send, sib_recv, (row, sibling, z))
    swap.start()

    loads[0].wait()

    def first(i, _):
        cut = pl.ds(pl.multiple_of(i * TILE, TILE), TILE)
        value = dot(x[half], inv[half, :, cut])
        p_rhs[:, cut] = value[:rows]
        p_left[:, cut] = value[rows:]
        return _

    lax.fori_loop(0, m // TILE, first, 0)
    loads[1].wait()
    far = x.at[1 - half]
    remote(far, far, sib_send, sib_recv, (row, sibling, z)).wait_recv()

    span_m = m // CHUNKS
    others = [lax.rem(z + step, nz) for step in range(1, nz)]

    def pieces(ch):
        return [
            remote(
                s_out.at[ch, other], s_in.at[ch, z], rs_send.at[ch, i], rs_recv.at[ch, z], (row, col, other)
            )
            for i, other in enumerate(others)
        ]

    def scatter(ch):
        for copy in pieces(ch):
            copy.start()

    def keep(ch, now):
        for zz in range(nz):
            s_out[ch, zz] = now[zz * slots:(zz + 1) * slots]

    partner = z + 1 - 2 * (z % 2)
    pairs = nz // 2

    def paired(ch):
        cut = pl.ds(ch * span_m, span_m)
        return remote(p_low.at[:, cut], w_in.at[:, cut], w_send.at[ch], w_recv.at[ch], (row, col, partner))

    for ch in range(CHUNKS):
        cut = slice(ch * span_m, (ch + 1) * span_m)
        value = dot(x[1 - half], inv[1 - half, :, cut])
        now = p_rhs[:, cut] + value[:rows]
        p_rhs[:, cut] = now
        p_low[:, cut] = (p_left[:, cut] + value[rows:]).astype(BF16)

        @pl.when(row > 0)
        def _():
            paired(ch).start()
            keep(ch, now.astype(BF16))

    @pl.when(row > 0)
    def _():
        for ch in range(CHUNKS):
            scatter(ch)
    swap.wait_send()

    fold = rows // 2
    piece = fold // nc
    for t in range(nb):
        later = nb - 1 - t
        wide = 2 * later * width

        @pl.when(row == t)
        def _():
            if t > 0:
                for ch in range(CHUNKS):
                    cut = slice(ch * span_m, (ch + 1) * span_m)
                    paired(ch).wait_recv()
                    p_sum[:, cut] = (p_low[:, cut].astype(F32) + w_in[:, cut].astype(F32)).astype(BF16)
            blocks = []
            for q in range(nb - 1):
                j = (t + 1 + q) % nb
                if j > t:
                    for zz in range(nz):
                        spot = oc_in.at[j, zz]
                        remote(spot, spot, ob_send.at[0, 0], ob_recv.at[j, zz], (j, col, zz)).wait_recv()
                    blocks.append(
                        jnp.concatenate(
                            [oc_in[j, zz][:, t * width:(t + 1) * width] for zz in range(nz)], axis=0
                        )
                    )
                else:
                    span = 2 * (nb - 1 - j) * width
                    sums = []
                    for c in range(nc):
                        total = None
                        for zz in range(nz):
                            spot = nc_in.at[j, c, zz, :, pl.ds(0, span)]
                            remote(
                                spot, spot, nb_send.at[0, 0, 0], nb_recv.at[j, c, zz], (j, c, zz)
                            ).wait_recv()
                            term = nc_in[j, c, zz, :, :span]
                            total = term if total is None else total + term
                        sums.append(total)
                    folded = jnp.concatenate(sums, axis=0)
                    at = (t - 1 - j) * width
                    whole = jnp.concatenate(
                        [folded[:, at:at + width], folded[:, span // 2 + at:span // 2 + at + width]], axis=0
                    )
                    lane = lax.broadcasted_iota(jnp.int32, whole.shape, 1)
                    whole = jnp.where(lane < ranks_ref[t, j], whole, jnp.zeros_like(whole))
                    blocks.append(whole.astype(BF16))
            coefs = blocks[0] if nb == 2 else jnp.concatenate(blocks, axis=1)
            value = None
            if t == 0 or later:
                for ch in range(CHUNKS):
                    cut = slice(ch * span_m, (ch + 1) * span_m)
                    now = p_rhs[:, cut] - dot(coefs, p_low[:, cut])
                    if t == 0:
                        p_rhs[:, cut] = now
                    now = now.astype(BF16)
                    if t == 0:
                        keep(ch, now)
                    if later:
                        term = dot_t(now, right_v[t + 1:, :, cut].reshape(later * width, span_m))
                        value = term if value is None else value + term
            if t > 0:
                coef_v[...] = coefs
            if later:
                folded = jnp.concatenate([value[:fold], value[fold:]], axis=1)
                for c in range(nc):
                    nc_part[c, :, :wide] = folded[c * piece:(c + 1) * piece]

        if later:
            for step in range(1, nc):
                other = lax.rem(col + step, nc)
                start(
                    row == t,
                    remote(
                        nc_part.at[other, :, pl.ds(0, wide)], nc_recv.at[col, :, pl.ds(0, wide)],
                        ng_send.at[step - 1], ng_recv.at[col], (row, other, z),
                    ),
                )
        if later:
            @pl.when(row == t)
            def _():
                total = nc_part[col, :, :wide]
                for step in range(1, nc):
                    other = lax.rem(col + step, nc)
                    spot = nc_recv.at[other, :, pl.ds(0, wide)]
                    remote(spot, spot, ng_send.at[0], ng_recv.at[other], (row, other, z)).wait_recv()
                    total = total + nc_recv[other, :, :wide]
                nc_sum[:, :wide] = total
            for i in range(t + 1, nb):
                for c in range(nc):
                    for zz in range(nz):
                        start(
                            row == t,
                            remote(
                                nc_sum.at[:, pl.ds(0, wide)], nc_in.at[t, col, z, :, pl.ds(0, wide)],
                                nb_send.at[i, c, zz], nb_recv.at[t, col, z], (i, c, zz),
                            ),
                        )


    @pl.when(row == 0)
    def _():
        for ch in range(CHUNKS):
            scatter(ch)

    @pl.when(row > 0)
    def _():
        spots = [lax.rem(z + 2 * k, nz) for k in range(pairs)]
        picked = jnp.concatenate(
            [coef_v[pl.ds(pl.multiple_of(spot * slots, slots), slots)] for spot in spots], axis=0
        )

        def across(k, ch):
            return remote(
                f_out.at[k - 1, ch], f_in.at[k - 1, ch], f_send.at[k - 1, ch], f_recv.at[k - 1, ch],
                (row, col, spots[k]),
            )

        for ch in range(CHUNKS):
            cut = slice(ch * span_m, (ch + 1) * span_m)
            value = dot(picked, p_sum[:, cut])
            for k in range(1, pairs):
                f_out[k - 1, ch] = value[k * slots:(k + 1) * slots].astype(BF16)
                across(k, ch).start()
            p_rhs[mine, cut] = p_rhs[mine, cut] - value[:slots]
        for ch in range(CHUNKS):
            cut = slice(ch * span_m, (ch + 1) * span_m)
            for k in range(1, pairs):
                across(k, ch).wait()
                p_rhs[mine, cut] = p_rhs[mine, cut] - f_in[k - 1, ch].astype(F32)
            paired(ch).wait_send()

    for ch in range(CHUNKS):
        cut = slice(ch * span_m, (ch + 1) * span_m)
        total = p_rhs[mine, cut]
        for other in others:
            spot = s_in.at[ch, other]
            remote(spot, spot, rs_send.at[0, 0], rs_recv.at[ch, other], (row, col, other)).wait_recv()
            total = total + s_in[ch, other].astype(F32)
        out_ref[0, :, cut] = total
    for ch in range(CHUNKS):
        for copy in pieces(ch):
            copy.wait_send()
    for pred, copy in sent:
        @pl.when(pred)
        def _():
            copy.wait_send()


def solution(mesh):
    nb, nc, nz = mesh.shape["row"], mesh.shape["col"], mesh.shape["rhs"]

    def body(right_side, guess, inverse, left_factor, right_factor, ranks):
        slots, m = right_side.shape[1:]
        width = left_factor.shape[2]
        rows = nz * slots
        part = inverse.shape[1] // 2
        deep = rows + (nb - 1) * width
        piece = rows // 2 // nc
        wide = 2 * (nb - 1) * width
        dma = pltpu.SemaphoreType.DMA
        hbm = pl.BlockSpec(memory_space=pltpu.HBM)
        vmem = pl.BlockSpec(memory_space=pltpu.VMEM)
        return pl.pallas_call(
            functools.partial(kernel, nb, nc, nz, width),
            out_shape=jax.ShapeDtypeStruct(right_side.shape, F32),
            in_specs=[
                hbm, hbm, hbm, hbm, hbm,
                pl.BlockSpec(memory_space=pltpu.SMEM),
            ],
            out_specs=vmem,
            scratch_shapes=[
                pltpu.VMEM((2, part, m), BF16),
                pltpu.VMEM((slots, m), F32),
                pltpu.VMEM((slots, m), F32),
                pltpu.VMEM((nb, width, m), BF16),
                pltpu.VMEM((2, slots, part), BF16),
                pltpu.VMEM((2, deep, part), BF16),
                pltpu.VMEM((rows, m), F32),
                pltpu.VMEM((deep - rows, m), F32),
                pltpu.VMEM((deep - rows, m), BF16),
                pltpu.VMEM((deep - rows, m), BF16),
                pltpu.VMEM((deep - rows, m), BF16),
                pltpu.VMEM((rows, deep - rows), BF16),
                pltpu.VMEM((nz // 2 - 1, CHUNKS, slots, m // CHUNKS), BF16),
                pltpu.VMEM((nz // 2 - 1, CHUNKS, slots, m // CHUNKS), BF16),
                pltpu.VMEM((nc, slots, nb * width), F32),
                pltpu.VMEM((slots, nb * width), BF16),
                pltpu.VMEM((nb, nz, slots, nb * width), BF16),
                pltpu.VMEM((nc, piece, wide), F32),
                pltpu.VMEM((nc, piece, wide), F32),
                pltpu.VMEM((piece, wide), F32),
                pltpu.VMEM((nb, nc, nz, piece, wide), F32),
                pltpu.VMEM((CHUNKS, nz, slots, m // CHUNKS), BF16),
                pltpu.VMEM((CHUNKS, nz, slots, m // CHUNKS), BF16),
                dma((2,)), dma((3,)), dma((nb - 1,)),
                dma((nc,)), dma((nz,)),
                dma((nb - 1, nc)), dma((nb - 1,)),
                dma, dma,
                dma((nc - 1,)), dma((nc,)),
                dma((nb - 1, nz)), dma((nb, nz)),
                dma((nc - 1,)), dma((nc,)),
                dma((nb, nc, nz)), dma((nb, nc, nz)),
                dma((CHUNKS, nz - 1)), dma((CHUNKS, nz)),
                dma((CHUNKS,)), dma((CHUNKS,)),
                dma((nz // 2 - 1, CHUNKS)), dma((nz // 2 - 1, CHUNKS)),
            ],
            compiler_params=pltpu.CompilerParams(
                collective_id=0, has_side_effects=True, vmem_limit_bytes=60 * 1024 * 1024
            ),
        )(right_side, guess, inverse, left_factor, right_factor, ranks)

    in_specs = (
        P("row", "rhs", "col"),
        P("row", "rhs", "col"),
        P("row", "rhs", "col"),
        P("row", None, None, "col"),
        P("row", None, None, "col"),
        P(),
    )
    out_specs = P("row", "rhs", "col")
    return jax.shard_map(body, mesh=mesh, in_specs=in_specs, out_specs=out_specs, check_vma=False)
```

```python
import functools

import jax
import jax.numpy as jnp
from jax import lax
from jax.experimental import pallas as pl
from jax.experimental.pallas import tpu as pltpu
from jax.sharding import PartitionSpec as P

F32 = jnp.float32
BF16 = jnp.bfloat16
TILE = 512
CHUNKS = 2


def dot(a, b):
    return lax.dot_general(a, b, (((1,), (0,)), ((), ())), preferred_element_type=F32)


def dot_t(a, b):
    return lax.dot_general(a, b, (((1,), (1,)), ((), ())), preferred_element_type=F32)


def kernel(
    nb, nc, nz, width,
    rhs_ref, guess_ref, inv_ref, left_ref, right_ref, ranks_ref, out_ref,
    inv, rhs_v, guess_v, right_v, low, x, p_rhs, p_left, p_low, p_sum, w_in,
    coef_v, f_out, f_in, oc_part, oc_sum, oc_in, nc_part, nc_recv, nc_sum, nc_in,
    s_out, s_in,
    inv_sem, in_sem, own_sem, rhs_send, rhs_recv, left_send, left_recv, sib_send, sib_recv,
    og_send, og_recv, ob_send, ob_recv, ng_send, ng_recv, nb_send, nb_recv, rs_send, rs_recv,
    w_send, w_recv, f_send, f_recv,
):
    row, col, z = lax.axis_index("row"), lax.axis_index("col"), lax.axis_index("rhs")
    slots, part = low.shape[1:]
    m = inv.shape[2]
    rows = nz * slots
    half = col % 2
    sibling = col + 1 - 2 * half
    diag = col == z
    sent = []

    def remote(src, dst, send, recv, where):
        return pltpu.make_async_remote_copy(
            src_ref=src, dst_ref=dst, send_sem=send, recv_sem=recv,
            device_id=where, device_id_type=pl.DeviceIdType.MESH,
        )

    def start(pred, copy):
        @pl.when(pred)
        def _():
            copy.start()
        sent.append((pred, copy))

    barrier = pltpu.get_barrier_semaphore()
    peers = [
        (row, lax.rem(col + dc, nc), lax.rem(z + dz, nz)) for dc in range(nc) for dz in range(nz) if dc or dz
    ] + [(lax.rem(row + dr, nb), col, lax.rem(z + dz, nz)) for dr in range(1, nb) for dz in range(nz)]
    for peer in peers:
        pl.semaphore_signal(barrier, inc=1, device_id=peer, device_id_type=pl.DeviceIdType.MESH)
    early = [
        pltpu.make_async_copy(src, dst, in_sem.at[i])
        for i, (src, dst) in enumerate(
            ((rhs_ref.at[0], rhs_v), (guess_ref.at[0], guess_v), (right_ref.at[0], right_v))
        )
    ]
    for load in early:
        load.start()
    loads = []
    for order in range(2):
        h = half if order == 0 else 1 - half
        load = pltpu.make_async_copy(
            inv_ref.at[0, pl.ds(pl.multiple_of(h * part, part), part)], inv.at[h], inv_sem.at[order]
        )
        load.start()
        loads.append(load)

    early[0].wait()
    for h in range(2):
        low[h] = rhs_v[:, h * part:(h + 1) * part].astype(BF16)
    early[1].wait()
    early[2].wait()
    coef = dot_t(guess_v[...].astype(BF16), right_v[...].reshape(nb * width, m))
    oc_part[col] = coef
    pl.semaphore_wait(barrier, len(peers))

    for step in range(1, nc):
        other = lax.rem(col + step, nc)
        start(
            row > 0,
            remote(oc_part.at[col], oc_part.at[col], og_send.at[step - 1], og_recv.at[col], (row, other, z)),
        )

    mine = pl.ds(pl.multiple_of(z * slots, slots), slots)
    for c in range(nc):
        start(
            jnp.logical_not(diag & (col == c)),
            remote(low.at[c % 2], x.at[c % 2, mine], rhs_send.at[c], rhs_recv.at[z], (row, c, col)),
        )
    for q in range(nb - 1):
        block = lax.rem(row + 1 + q, nb)
        spot = pl.ds(rows + q * width, width)
        for c in range(nc):
            start(
                diag & (col != c),
                remote(
                    left_ref.at[0, block, :, pl.ds((c % 2) * part, part)],
                    x.at[c % 2, spot], left_send.at[q, c], left_recv.at[q], (row, c, z),
                ),
            )
    def own(q):
        return pltpu.make_async_copy(
            left_ref.at[0, lax.rem(row + 1 + q, nb), :, pl.ds(pl.multiple_of(half * part, part), part)],
            x.at[half, pl.ds(rows + q * width, width)], own_sem.at[q],
        )

    @pl.when(diag)
    def _():
        for q in range(nb - 1):
            own(q).start()
        x[half, mine] = low[half]

    @pl.when(row > 0)
    def _():
        total = oc_part[col]
        for step in range(1, nc):
            other = lax.rem(col + step, nc)
            remote(
                oc_part.at[other], oc_part.at[other], og_send.at[step - 1], og_recv.at[other], (row, other, z)
            ).wait_recv()
            total = total + oc_part[other]
        lane = lax.broadcasted_iota(jnp.int32, total.shape, 1)
        kept = jnp.zeros_like(total)
        for i in range(nb):
            inside = (lane >= i * width) & (lane < i * width + ranks_ref[i, row])
            kept = jnp.where(inside, total, kept)
        oc_sum[...] = kept.astype(BF16)
    for i in range(nb - 1):
        for zz in range(nz):
            start(
                row > i,
                remote(oc_sum, oc_in.at[row, z], ob_send.at[i, zz], ob_recv.at[row, z], (i, col, zz)),
            )

    for zz in range(nz):
        @pl.when(jnp.logical_not(diag & (z == zz)))
        def _():
            spot = x.at[half, pl.ds(zz * slots, slots)]
            remote(spot, spot, rhs_send.at[0], rhs_recv.at[zz], (row, sibling, z)).wait_recv()

    @pl.when(diag)
    def _():
        for q in range(nb - 1):
            own(q).wait()

    @pl.when(jnp.logical_not(diag))
    def _():
        for q in range(nb - 1):
            spot = x.at[half, pl.ds(rows + q * width, width)]
            remote(spot, spot, left_send.at[0, 0], left_recv.at[q], (row, sibling, z)).wait_recv()

    swap = remote(x.at[half], x.at[half], sib_send, sib_recv, (row, sibling, z))
    swap.start()

    loads[0].wait()

    def first(i, _):
        cut = pl.ds(pl.multiple_of(i * TILE, TILE), TILE)
        value = dot(x[half], inv[half, :, cut])
        p_rhs[:, cut] = value[:rows]
        p_left[:, cut] = value[rows:]
        return _

    lax.fori_loop(0, m // TILE, first, 0)
    loads[1].wait()
    far = x.at[1 - half]
    remote(far, far, sib_send, sib_recv, (row, sibling, z)).wait_recv()

    span_m = m // CHUNKS
    others = [lax.rem(z + step, nz) for step in range(1, nz)]

    def pieces(ch):
        return [
            remote(
                s_out.at[ch, other], s_in.at[ch, z], rs_send.at[ch, i], rs_recv.at[ch, z], (row, col, other)
            )
            for i, other in enumerate(others)
        ]

    def scatter(ch):
        for copy in pieces(ch):
            copy.start()

    def keep(ch, now):
        for zz in range(nz):
            s_out[ch, zz] = now[zz * slots:(zz + 1) * slots]

    partner = z + 1 - 2 * (z % 2)
    pairs = nz // 2

    def paired(ch):
        cut = pl.ds(ch * span_m, span_m)
        return remote(p_low.at[:, cut], w_in.at[:, cut], w_send.at[ch], w_recv.at[ch], (row, col, partner))

    for ch in range(CHUNKS):
        cut = slice(ch * span_m, (ch + 1) * span_m)
        value = dot(x[1 - half], inv[1 - half, :, cut])
        now = p_rhs[:, cut] + value[:rows]
        p_rhs[:, cut] = now
        p_low[:, cut] = (p_left[:, cut] + value[rows:]).astype(BF16)

        @pl.when(row > 0)
        def _():
            paired(ch).start()
            keep(ch, now.astype(BF16))

    @pl.when(row > 0)
    def _():
        for ch in range(CHUNKS):
            scatter(ch)
    swap.wait_send()

    fold = rows // 2
    for t in range(nb):
        later = nb - 1 - t
        wide = 2 * later * width

        @pl.when(row == t)
        def _():
            if t > 0:
                for ch in range(CHUNKS):
                    cut = slice(ch * span_m, (ch + 1) * span_m)
                    paired(ch).wait_recv()
                    p_sum[:, cut] = (p_low[:, cut].astype(F32) + w_in[:, cut].astype(F32)).astype(BF16)
            blocks = []
            for q in range(nb - 1):
                j = (t + 1 + q) % nb
                if j > t:
                    for zz in range(nz):
                        spot = oc_in.at[j, zz]
                        remote(spot, spot, ob_send.at[0, 0], ob_recv.at[j, zz], (j, col, zz)).wait_recv()
                    blocks.append(
                        jnp.concatenate(
                            [oc_in[j, zz][:, t * width:(t + 1) * width] for zz in range(nz)], axis=0
                        )
                    )
                else:
                    span = 2 * (nb - 1 - j) * width
                    folded = None
                    for zz in range(nz):
                        spot = nc_in.at[j, zz, :, pl.ds(0, span)]
                        remote(spot, spot, nb_send.at[0, 0], nb_recv.at[j, zz], (j, col, zz)).wait_recv()
                        term = nc_in[j, zz, :, :span]
                        folded = term if folded is None else folded + term
                    at = (t - 1 - j) * width
                    whole = jnp.concatenate(
                        [folded[:, at:at + width], folded[:, span // 2 + at:span // 2 + at + width]], axis=0
                    )
                    lane = lax.broadcasted_iota(jnp.int32, whole.shape, 1)
                    whole = jnp.where(lane < ranks_ref[t, j], whole, jnp.zeros_like(whole))
                    blocks.append(whole.astype(BF16))
            coefs = blocks[0] if nb == 2 else jnp.concatenate(blocks, axis=1)
            value = None
            if t == 0 or later:
                for ch in range(CHUNKS):
                    cut = slice(ch * span_m, (ch + 1) * span_m)
                    now = p_rhs[:, cut] - dot(coefs, p_low[:, cut])
                    if t == 0:
                        p_rhs[:, cut] = now
                    now = now.astype(BF16)
                    if t == 0:
                        keep(ch, now)
                    if later:
                        term = dot_t(now, right_v[t + 1:, :, cut].reshape(later * width, span_m))
                        value = term if value is None else value + term
            if t > 0:
                coef_v[...] = coefs
            if later:
                folded = jnp.concatenate([value[:fold], value[fold:]], axis=1)
                nc_part[:, :wide] = folded

        if later:
            for step in range(1, nc):
                other = lax.rem(col + step, nc)
                start(
                    row == t,
                    remote(
                        nc_part.at[:, pl.ds(0, wide)], nc_recv.at[col, :, pl.ds(0, wide)],
                        ng_send.at[step - 1], ng_recv.at[col], (row, other, z),
                    ),
                )
        if later:
            @pl.when(row == t)
            def _():
                total = nc_part[:, :wide]
                for step in range(1, nc):
                    other = lax.rem(col + step, nc)
                    spot = nc_recv.at[other, :, pl.ds(0, wide)]
                    remote(spot, spot, ng_send.at[0], ng_recv.at[other], (row, other, z)).wait_recv()
                    total = total + nc_recv[other, :, :wide]
                nc_sum[:, :wide] = total
            for i in range(t + 1, nb):
                for zz in range(nz):
                    start(
                        row == t,
                        remote(
                            nc_sum.at[:, pl.ds(0, wide)], nc_in.at[t, z, :, pl.ds(0, wide)],
                            nb_send.at[i, zz], nb_recv.at[t, z], (i, col, zz),
                        ),
                    )

    @pl.when(row == 0)
    def _():
        for ch in range(CHUNKS):
            scatter(ch)

    @pl.when(row > 0)
    def _():
        spots = [lax.rem(z + 2 * k, nz) for k in range(pairs)]
        picked = jnp.concatenate(
            [coef_v[pl.ds(pl.multiple_of(spot * slots, slots), slots)] for spot in spots], axis=0
        )

        def across(k, ch):
            return remote(
                f_out.at[k - 1, ch], f_in.at[k - 1, ch], f_send.at[k - 1, ch], f_recv.at[k - 1, ch],
                (row, col, spots[k]),
            )

        for ch in range(CHUNKS):
            cut = slice(ch * span_m, (ch + 1) * span_m)
            value = dot(picked, p_sum[:, cut])
            for k in range(1, pairs):
                f_out[k - 1, ch] = value[k * slots:(k + 1) * slots].astype(BF16)
                across(k, ch).start()
            p_rhs[mine, cut] = p_rhs[mine, cut] - value[:slots]
        for ch in range(CHUNKS):
            cut = slice(ch * span_m, (ch + 1) * span_m)
            for k in range(1, pairs):
                across(k, ch).wait()
                p_rhs[mine, cut] = p_rhs[mine, cut] - f_in[k - 1, ch].astype(F32)
            paired(ch).wait_send()

    for ch in range(CHUNKS):
        cut = slice(ch * span_m, (ch + 1) * span_m)
        total = p_rhs[mine, cut]
        for other in others:
            spot = s_in.at[ch, other]
            remote(spot, spot, rs_send.at[0, 0], rs_recv.at[ch, other], (row, col, other)).wait_recv()
            total = total + s_in[ch, other].astype(F32)
        out_ref[0, :, cut] = total
    for ch in range(CHUNKS):
        for copy in pieces(ch):
            copy.wait_send()
    for pred, copy in sent:
        @pl.when(pred)
        def _():
            copy.wait_send()


def solution(mesh):
    nb, nc, nz = mesh.shape["row"], mesh.shape["col"], mesh.shape["rhs"]

    def body(right_side, guess, inverse, left_factor, right_factor, ranks):
        slots, m = right_side.shape[1:]
        width = left_factor.shape[2]
        rows = nz * slots
        part = inverse.shape[1] // 2
        deep = rows + (nb - 1) * width
        wide = 2 * (nb - 1) * width
        dma = pltpu.SemaphoreType.DMA
        hbm = pl.BlockSpec(memory_space=pltpu.HBM)
        vmem = pl.BlockSpec(memory_space=pltpu.VMEM)
        return pl.pallas_call(
            functools.partial(kernel, nb, nc, nz, width),
            out_shape=jax.ShapeDtypeStruct(right_side.shape, F32),
            in_specs=[
                hbm, hbm, hbm, hbm, hbm,
                pl.BlockSpec(memory_space=pltpu.SMEM),
            ],
            out_specs=vmem,
            scratch_shapes=[
                pltpu.VMEM((2, part, m), BF16),
                pltpu.VMEM((slots, m), F32),
                pltpu.VMEM((slots, m), F32),
                pltpu.VMEM((nb, width, m), BF16),
                pltpu.VMEM((2, slots, part), BF16),
                pltpu.VMEM((2, deep, part), BF16),
                pltpu.VMEM((rows, m), F32),
                pltpu.VMEM((deep - rows, m), F32),
                pltpu.VMEM((deep - rows, m), BF16),
                pltpu.VMEM((deep - rows, m), BF16),
                pltpu.VMEM((deep - rows, m), BF16),
                pltpu.VMEM((rows, deep - rows), BF16),
                pltpu.VMEM((nz // 2 - 1, CHUNKS, slots, m // CHUNKS), BF16),
                pltpu.VMEM((nz // 2 - 1, CHUNKS, slots, m // CHUNKS), BF16),
                pltpu.VMEM((nc, slots, nb * width), F32),
                pltpu.VMEM((slots, nb * width), BF16),
                pltpu.VMEM((nb, nz, slots, nb * width), BF16),
                pltpu.VMEM((rows // 2, wide), F32),
                pltpu.VMEM((nc, rows // 2, wide), F32),
                pltpu.VMEM((rows // 2, wide), F32),
                pltpu.VMEM((nb, nz, rows // 2, wide), F32),
                pltpu.VMEM((CHUNKS, nz, slots, m // CHUNKS), BF16),
                pltpu.VMEM((CHUNKS, nz, slots, m // CHUNKS), BF16),
                dma((2,)), dma((3,)), dma((nb - 1,)),
                dma((nc,)), dma((nz,)),
                dma((nb - 1, nc)), dma((nb - 1,)),
                dma, dma,
                dma((nc - 1,)), dma((nc,)),
                dma((nb - 1, nz)), dma((nb, nz)),
                dma((nc - 1,)), dma((nc,)),
                dma((nb, nz)), dma((nb, nz)),
                dma((CHUNKS, nz - 1)), dma((CHUNKS, nz)),
                dma((CHUNKS,)), dma((CHUNKS,)),
                dma((nz // 2 - 1, CHUNKS)), dma((nz // 2 - 1, CHUNKS)),
            ],
            compiler_params=pltpu.CompilerParams(
                collective_id=0, has_side_effects=True, vmem_limit_bytes=60 * 1024 * 1024
            ),
        )(right_side, guess, inverse, left_factor, right_factor, ranks)

    in_specs = (
        P("row", "rhs", "col"),
        P("row", "rhs", "col"),
        P("row", "rhs", "col"),
        P("row", None, None, "col"),
        P("row", None, None, "col"),
        P(),
    )
    out_specs = P("row", "rhs", "col")
    return jax.shard_map(body, mesh=mesh, in_specs=in_specs, out_specs=out_specs, check_vma=False)
```
